32 devices in a mesh: row: 8 (over y, x, core), col: 4 (over z).
Axes of the slice: x: 2, y: 2, z: 4, core: 2. Of those that a mesh axis runs over, the one named last changes fastest.
Arguments:
- pair: bfloat16 [64, 64, 128], P('row', 'col'), may hold values from -6 to 6
- pair_mask: int32 [64, 64], P('row', 'col'), may hold values 0 or 1
- ln_in_gain: float32 [128], replicated, may hold values from 0.1 to 1.9
- ln_in_bias: float32 [128], replicated, may hold values from -3 to 3
- w_proj: bfloat16 [128, 512], replicated, may hold values from -0.5 to 0.5
- b_proj: float32 [512], replicated, may hold values from -3 to 3
- w_gate: bfloat16 [128, 128], replicated, may hold values from -0.5 to 0.5
- b_gate: float32 [128], replicated, may hold values from -3 to 3
- ln_mid_gain: float32 [128], replicated, may hold values from 0.1 to 1.9
- ln_mid_bias: float32 [128], replicated, may hold values from -3 to 3
- w_out: bfloat16 [128, 128], replicated, may hold values from -0.5 to 0.5
- b_out: float32 [128], replicated, may hold values from -3 to 3
- cotangent: bfloat16 [64, 64, 128], P('row', 'col'), may hold values from -6 to 6
Outputs:
- update: bfloat16 [64, 64, 128], P('row', 'col')
- pair_grad: float32 [64, 64, 128], P('row', 'col')
The draws below stay inside these ranges and needn't reach their ends.
All inputs are finite; a program needn't handle non-finite values. No bound on the sum of `pair_mask` on one device may be relied on, other than what follows from the above.
Results may differ from the reference program's by a relative error of at most 0.019.
Values may be sent and summed in bfloat16 or wider, within the bound.
A program may use at most 64 MiB of HBM per device.

```python
import jax
import jax.numpy as jnp
from jax import lax

C = 128
H = 128
TILE_I = 8
N = 64
N_ROW = 8


def set_ends(entries, key, low, top_value):
    index_at = [jax.random.randint(jax.random.fold_in(key, axis), (), 0, length) for axis, length in enumerate(entries.shape)]
    widest = entries.shape.index(max(entries.shape))
    neighbour = index_at[:widest] + [(index_at[widest] + 1) % entries.shape[widest]] + index_at[widest + 1:]
    return entries.at[tuple(index_at)].set(low).at[tuple(neighbour)].set(top_value)


def block_levels(stream_key, shape, shards, low, top_value):
    def one(position, parts):
        steps = jax.random.uniform(jax.random.fold_in(jax.random.fold_in(stream_key, 6), position), (parts,), jnp.float32, low / len(shards), top_value / len(shards))
        return jnp.repeat(jnp.exp(steps), shape[position] // parts).reshape((-1,) + (1,) * (len(shape) - position - 1))

    level = one(*shards[0])
    for cut in shards[1:]:
        level = level * one(*cut)
    return level


def normal_values(key, shape, spread, reach, pieces=(), dtype=jnp.bfloat16):
    array = jax.random.normal(key, shape, jnp.float32) * spread
    if len(pieces) > 0:
        array = block_levels(key, shape, pieces, -0.22, 0.18) * array
    return jnp.clip(array, min=-reach, max=reach).astype(dtype)


def setup_inputs(seed: int = 0) -> dict:
    seeds = jax.random.split(jax.random.key(seed), 14)
    pair = normal_values(seeds[0], (N, N, C), 1.0, 6.0, ((0, 8), (1, 4)))
    pair_mask = set_ends((jax.random.randint(seeds[1], (N, N), 0, 8) < 7).astype(jnp.int32), jax.random.fold_in(seeds[1], 1), 0, 1)
    ln_in_gain = jnp.clip(1.0 + 0.18 * jax.random.normal(seeds[2], (C,), jnp.float32), 0.1, 1.9)
    ln_in_bias = normal_values(seeds[3], (C,), 0.5, 3.0, (), jnp.float32)
    w_proj = normal_values(seeds[4], (C, 4 * H), C ** -0.5, 0.5)
    b_proj = normal_values(seeds[5], (4 * H,), 0.5, 3.0, (), jnp.float32)
    w_gate = normal_values(seeds[6], (C, C), C ** -0.5, 0.5)
    b_gate = normal_values(seeds[7], (C,), 0.5, 3.0, (), jnp.float32)
    ln_mid_gain = jnp.clip(1.0 + 0.18 * jax.random.normal(seeds[8], (H,), jnp.float32), 0.1, 1.9)
    ln_mid_bias = normal_values(seeds[9], (H,), 0.5, 3.0, (), jnp.float32)
    w_out = normal_values(seeds[10], (H, C), H ** -0.5, 0.5)
    b_out = normal_values(seeds[11], (C,), 0.5, 3.0, (), jnp.float32)
    cotangent = normal_values(seeds[12], (N, N, C), 1.0, 6.0, ((0, 8), (1, 4)))
    return dict(pair=pair, pair_mask=pair_mask, ln_in_gain=ln_in_gain, ln_in_bias=ln_in_bias, w_proj=w_proj, b_proj=b_proj, w_gate=w_gate, b_gate=b_gate, ln_mid_gain=ln_mid_gain, ln_mid_bias=ln_mid_bias, w_out=w_out, b_out=b_out, cotangent=cotangent)


def layer_norm(values, gain_vec, bias_vec):
    average = lax.optimization_barrier(jnp.mean(values, -1, keepdims=True))
    centred = values - average
    inv_std = lax.rsqrt(lax.optimization_barrier(jnp.mean(centred * centred, -1, keepdims=True)) + 1e-05)
    hat_val = centred * inv_std
    return (hat_val * gain_vec + bias_vec, hat_val, inv_std)

def norm_back(upstream, hat_val, inv_std, gain_vec):
    scaled = upstream * gain_vec
    return inv_std * (scaled - lax.optimization_barrier(jnp.mean(scaled, -1, keepdims=True)) - hat_val * lax.optimization_barrier(jnp.mean(scaled * hat_val, -1, keepdims=True)))

def gate_pair(proj, mask_f):
    hidden = proj.shape[-1] // 4
    sig_a = jax.nn.sigmoid(proj[..., :hidden])
    sig_b = jax.nn.sigmoid(proj[..., 2 * hidden:3 * hidden])
    a_bf = (mask_f * sig_a * proj[..., hidden:2 * hidden]).astype(jnp.bfloat16)
    b_bf = (mask_f * sig_b * proj[..., 3 * hidden:]).astype(jnp.bfloat16)
    return (a_bf, b_bf)

def gate_back(grad_a, grad_b, proj, mask_f):
    hidden = proj.shape[-1] // 4
    sig_a = jax.nn.sigmoid(proj[..., :hidden])
    val_a = proj[..., hidden:2 * hidden]
    sig_b = jax.nn.sigmoid(proj[..., 2 * hidden:3 * hidden])
    val_b = proj[..., 3 * hidden:]
    masked_a = grad_a * mask_f
    masked_b = grad_b * mask_f
    return jnp.concatenate([masked_a * val_a * sig_a * (1.0 - sig_a), masked_a * sig_a, masked_b * val_b * sig_b * (1.0 - sig_b), masked_b * sig_b], -1)

def reference(pair, pair_mask, ln_in_gain, ln_in_bias, w_proj, b_proj, w_gate, b_gate, ln_mid_gain, ln_mid_bias, w_out, b_out, cotangent):
    normed, hat_in, rstd_in = layer_norm(pair.astype(jnp.float32), ln_in_gain, ln_in_bias)
    x_bf = normed.astype(jnp.bfloat16)
    proj = jnp.dot(x_bf, w_proj, preferred_element_type=jnp.float32) + b_proj
    mask_f = pair_mask.astype(jnp.float32)[..., None]
    a_bf, b_bf = gate_pair(proj, mask_f)
    triangle = jnp.einsum('ikh,jkh->ijh', a_bf.astype(jnp.float32), b_bf.astype(jnp.float32))
    mid_val, hat_mid, rstd_mid = layer_norm(triangle, ln_mid_gain, ln_mid_bias)
    mid_bf = mid_val.astype(jnp.bfloat16)
    out_lin = jnp.dot(mid_bf, w_out, preferred_element_type=jnp.float32) + b_out
    gate = jax.nn.sigmoid(jnp.dot(x_bf, w_gate, preferred_element_type=jnp.float32) + b_gate)
    update = (gate * out_lin).astype(jnp.bfloat16)
    grad_out = cotangent.astype(jnp.float32)
    d_out = (grad_out * gate).astype(jnp.bfloat16)
    d_gpre = (grad_out * out_lin * gate * (1.0 - gate)).astype(jnp.bfloat16)
    d_mid = jnp.dot(d_out, w_out.T, preferred_element_type=jnp.float32)
    d_tri = norm_back(d_mid, hat_mid, rstd_mid, ln_mid_gain).astype(jnp.bfloat16)
    grad_a = jnp.einsum('ijh,jkh->ikh', d_tri.astype(jnp.float32), b_bf.astype(jnp.float32))
    total = N
    hidden = a_bf.shape[-1]
    tri_blocks = d_tri.reshape(N_ROW, TILE_I, total, hidden)
    a_blocks = a_bf.reshape(N_ROW, TILE_I, total, hidden)

    def add_block(running, blocks):
        tri_part, a_part = blocks
        partial_value = jnp.einsum('ijh,ikh->jkh', tri_part.astype(jnp.float32), a_part.astype(jnp.float32))
        rounded = lax.optimization_barrier(partial_value.astype(jnp.bfloat16))
        return (running + rounded.astype(jnp.float32), None)
    grad_b, _ = lax.scan(add_block, jnp.zeros((total, total, hidden), jnp.float32), (tri_blocks, a_blocks))
    d_proj = gate_back(grad_a, grad_b, proj, mask_f).astype(jnp.bfloat16)
    d_x = jnp.dot(d_proj, w_proj.T, preferred_element_type=jnp.float32) + jnp.dot(d_gpre, w_gate.T, preferred_element_type=jnp.float32)
    pair_grad = norm_back(d_x, hat_in, rstd_in, ln_in_gain)
    return (update, pair_grad)
```

```python
import functools

import jax
import jax.numpy as jnp
from jax import lax
from jax.experimental import pallas as pl
from jax.experimental.pallas import tpu as pltpu
from jax.sharding import PartitionSpec as P

F32 = jnp.float32
BF16 = jnp.bfloat16
MESH = pl.DeviceIdType.MESH


def flip(index, step, size):
    if size & (size - 1):
        return lax.rem(index + step, size)
    partner, weight = 0, 1
    while weight < size:
        mine, other = (index // weight) % 2, (step // weight) % 2
        partner = partner + weight * ((mine + other) % 2)
        weight *= 2
    return partner


def source(index, step, size):
    if size & (size - 1):
        return lax.rem(index + size - step, size)
    return flip(index, step, size)


def normalize(values):
    centred = values - jnp.mean(values, -1, keepdims=True)
    inv_std = lax.rsqrt(jnp.mean(centred * centred, -1, keepdims=True) + 1e-05)
    return centred * inv_std, inv_std


def norm_back(upstream, hat, inv_std, gain):
    scaled = upstream * gain
    return inv_std * (
        scaled
        - jnp.mean(scaled, -1, keepdims=True)
        - hat * jnp.mean(scaled * hat, -1, keepdims=True)
    )


def dot(lhs, rhs):
    return jnp.dot(lhs, rhs, preferred_element_type=F32)


def dot_t(lhs, rhs):
    return lax.dot_general(lhs, rhs, (((1,), (1,)), ((), ())), preferred_element_type=F32)


def kernel(
    n_row, n_col, ti, tj,
    pair_ref, mask_ref, gin_ref, bin_ref, wp_ref, bp_ref, wg_ref, bg_ref,
    gmid_ref, bmid_ref, wo_ref, bo_ref, cot_ref,
    upd_ref, grad_ref,
    stage, a_f, b_out, b_in, b_f, tri_own, tri_out, tri_in, d_out_s, d_in, d_f, gb_own, gb_out, gb_in,
    b_ss, b_rs, t_ss, t_rs, d_ss, d_rs, g_ss, g_rs,
):
    row, col = lax.axis_index("row"), lax.axis_index("col")
    tok = ti * tj
    half = ti * ti
    per = tj // ti
    hid = a_f.shape[-1]

    barrier = pltpu.get_barrier_semaphore()
    for step in range(1, n_row):
        pl.semaphore_signal(barrier, inc=1, device_id=(flip(row, step, n_row), col), device_id_type=MESH)
    for step in range(1, n_col):
        pl.semaphore_signal(barrier, inc=1, device_id=(row, flip(col, step, n_col)), device_id_type=MESH)

    def reorder(ref):
        stage[...] = ref[...].astype(F32).reshape(tok, hid)
        return jnp.concatenate([stage[pl.ds(k, ti, stride=tj), :] for k in range(tj)], 0)

    hat_in, rstd_in = normalize(reorder(pair_ref))
    x_bf = (hat_in * gin_ref[...] + bin_ref[...]).astype(BF16)
    proj = dot(x_bf, wp_ref[...]) + bp_ref[...]
    mask_v = mask_ref[...].astype(F32)
    mask = jnp.concatenate(
        [jnp.broadcast_to(mask_v[:, k : k + 1], (ti, hid)) for k in range(tj)], 0
    )
    sig_b = jax.nn.sigmoid(proj[:, 2 * hid : 3 * hid])
    val_b = proj[:, 3 * hid :]
    b_bf = (mask * sig_b * val_b).astype(BF16)
    b_out[...] = b_bf

    pl.semaphore_wait(barrier, n_row + n_col - 2)

    def send_b(step):
        to = flip(row, step, n_row)
        return pltpu.make_async_remote_copy(
            b_out, b_in.at[row], b_ss.at[step], b_rs.at[step],
            device_id=(to, col), device_id_type=MESH,
        )

    for step in range(n_row - 1, 0, -1):
        send_b(step).start()

    sig_a = jax.nn.sigmoid(proj[:, :hid])
    val_a = proj[:, hid : 2 * hid]
    a_f[...] = (mask * sig_a * val_a).astype(BF16).astype(F32)
    b_f[row] = b_bf.astype(F32)

    def send_tri(block):
        to = block // per
        part = block % per
        return pltpu.make_async_remote_copy(
            tri_out.at[block], tri_in.at[col, part], t_ss.at[block], t_rs.at[col, part],
            device_id=(row, to), device_id_type=MESH,
        )

    def forward(block):
        sums = []
        a_k = [a_f[k * ti : (k + 1) * ti, :] for k in range(tj)]
        for jj in range(ti):
            total = None
            for k in range(tj):
                term = a_k[k] * b_f[block, k * ti + jj : k * ti + jj + 1, :]
                total = term if total is None else total + term
            sums.append(total)
        whole = jnp.concatenate(sums, 0)

        @pl.when(block // per == col)
        def _():
            tri_own[block % per] = whole

        @pl.when(block // per != col)
        def _():
            tri_out[block] = whole.astype(BF16)
            send_tri(block).start()

    forward(row)

    def forward_step(step, carry):
        block = source(row, step, n_row)
        pltpu.make_async_remote_copy(
            b_out, b_in.at[block], b_ss.at[step], b_rs.at[step],
            device_id=(block, col), device_id_type=MESH,
        ).wait_recv()
        b_f[block] = b_in[block].astype(F32)
        forward(block)
        return carry

    lax.fori_loop(1, n_row, forward_step, 0)

    gate = jax.nn.sigmoid(dot(x_bf, wg_ref[...]) + bg_ref[...])
    grad_out = reorder(cot_ref)
    d_out = (grad_out * gate).astype(BF16)
    d_mid = dot_t(d_out, wo_ref[...])

    triangle = jnp.concatenate([tri_own[part] for part in range(per)], 0)
    for step in range(1, n_col):
        other = source(col, step, n_col)
        for part in range(per):
            pltpu.make_async_remote_copy(
                tri_out.at[0], tri_in.at[other, part], t_ss.at[0], t_rs.at[other, part],
                device_id=(row, other), device_id_type=MESH,
            ).wait_recv()
        triangle = triangle + jnp.concatenate(
            [tri_in[other, part].astype(F32) for part in range(per)], 0
        )
    hat_mid, rstd_mid = normalize(triangle)
    d_tri = norm_back(d_mid, hat_mid, rstd_mid, gmid_ref[...]).astype(BF16)
    d_out_s[...] = d_tri

    def send_d(step):
        to = flip(col, step, n_col)
        return pltpu.make_async_remote_copy(
            d_out_s, d_in.at[col], d_ss.at[step], d_rs.at[step],
            device_id=(row, to), device_id_type=MESH,
        )

    for step in range(n_col - 1, 0, -1):
        send_d(step).start()
    d_f[pl.ds(col * tok, tok), :] = d_tri.astype(F32)

    def send_gb(block):
        return pltpu.make_async_remote_copy(
            gb_out.at[block], gb_in.at[row], g_ss.at[block], g_rs.at[row],
            device_id=(block, col), device_id_type=MESH,
        )

    def backward_b(block):
        d_i = [d_f[pl.ds(block * half + i, ti, stride=ti), :] for i in range(ti)]
        sums = []
        for k in range(tj):
            total = None
            for i in range(ti):
                term = d_i[i] * a_f[k * ti + i : k * ti + i + 1, :]
                total = term if total is None else total + term
            sums.append(total)
        whole = jnp.concatenate(sums, 0)

        @pl.when(block == row)
        def _():
            gb_own[...] = whole

        @pl.when(block != row)
        def _():
            gb_out[block] = whole.astype(BF16)
            send_gb(block).start()

    for part in range(per):
        backward_b(col * per + part)

    mid_bf = (hat_mid * gmid_ref[...] + bmid_ref[...]).astype(BF16)
    out_lin = dot(mid_bf, wo_ref[...]) + bo_ref[...]
    update = gate * out_lin
    for k in range(tj):
        stage[pl.ds(k, ti, stride=tj), :] = update[k * ti : (k + 1) * ti, :]
    upd_ref[...] = stage[...].astype(BF16).reshape(ti, tj, hid)
    d_gpre = (grad_out * out_lin * gate * (1.0 - gate)).astype(BF16)

    def backward_step(step, carry):
        other = source(col, step, n_col)
        pltpu.make_async_remote_copy(
            d_out_s, d_in.at[other], d_ss.at[step], d_rs.at[step],
            device_id=(row, other), device_id_type=MESH,
        ).wait_recv()
        d_f[pl.ds(other * tok, tok), :] = d_in[other].astype(F32)
        for part in range(per):
            backward_b(other * per + part)
        return carry

    lax.fori_loop(1, n_col, backward_step, 0)

    def backward_a(block, sums):
        out = list(sums)
        for jj in range(ti):
            d_j = d_f[pl.ds(block * half + jj * ti, ti), :]
            for k in range(tj):
                out[k] = out[k] + d_j * b_f[block, k * ti + jj : k * ti + jj + 1, :]
        return tuple(out)

    zero = tuple(jnp.zeros((ti, hid), F32) for _ in range(tj))
    grad_a = jnp.concatenate(lax.fori_loop(0, n_row, backward_a, zero), 0) * mask
    d_ga = (grad_a * val_a * sig_a * (1.0 - sig_a)).astype(BF16)
    d_va = (grad_a * sig_a).astype(BF16)
    d_x = (
        dot_t(d_gpre, wg_ref[...])
        + dot_t(d_ga, wp_ref[:, :hid])
        + dot_t(d_va, wp_ref[:, hid : 2 * hid])
    )

    grad_b = gb_own[...]
    for step in range(1, n_row):
        other = source(row, step, n_row)
        pltpu.make_async_remote_copy(
            gb_out.at[0], gb_in.at[other], g_ss.at[0], g_rs.at[other],
            device_id=(other, col), device_id_type=MESH,
        ).wait_recv()
        grad_b = grad_b + gb_in[other].astype(F32)
    grad_b = grad_b * mask
    d_gb = (grad_b * val_b * sig_b * (1.0 - sig_b)).astype(BF16)
    d_vb = (grad_b * sig_b).astype(BF16)
    d_x = d_x + dot_t(d_gb, wp_ref[:, 2 * hid : 3 * hid]) + dot_t(d_vb, wp_ref[:, 3 * hid :])
    pair_grad = norm_back(d_x, hat_in, rstd_in, gin_ref[...])
    for k in range(tj):
        stage[pl.ds(k, ti, stride=tj), :] = pair_grad[k * ti : (k + 1) * ti, :]
    grad_ref[...] = stage[...].reshape(ti, tj, hid)

    for step in range(1, n_row):
        send_b(step).wait_send()
    for block in range(n_row):
        @pl.when(block // per != col)
        def _():
            send_tri(block).wait_send()
    for step in range(1, n_col):
        send_d(step).wait_send()
    for block in range(n_row):
        @pl.when(block != row)
        def _():
            send_gb(block).wait_send()


def per_device(n_row, n_col, pair, pair_mask, gin, bin_, wp, bp, wg, bg, gmid, bmid, wo, bo, cot):
    ti, tj, chan = pair.shape
    hid = chan
    tok, per = ti * tj, tj // ti
    vec = lambda v: v.reshape(1, -1)
    dma = pltpu.SemaphoreType.DMA
    vmem = pl.BlockSpec(memory_space=pltpu.VMEM)
    return pl.pallas_call(
        functools.partial(kernel, n_row, n_col, ti, tj),
        name="triangle_step",
        out_shape=(
            jax.ShapeDtypeStruct(pair.shape, BF16),
            jax.ShapeDtypeStruct(pair.shape, F32),
        ),
        in_specs=[vmem] * 13,
        out_specs=(vmem, vmem),
        scratch_shapes=[
            pltpu.VMEM((tok, hid), F32),
            pltpu.VMEM((tok, hid), F32),
            pltpu.VMEM((tok, hid), BF16),
            pltpu.VMEM((n_row, tok, hid), BF16),
            pltpu.VMEM((n_row, tok, hid), F32),
            pltpu.VMEM((per, ti * ti, hid), F32),
            pltpu.VMEM((n_row, ti * ti, hid), BF16),
            pltpu.VMEM((n_col, per, ti * ti, hid), BF16),
            pltpu.VMEM((tok, hid), BF16),
            pltpu.VMEM((n_col, tok, hid), BF16),
            pltpu.VMEM((n_col * tok, hid), F32),
            pltpu.VMEM((tok, hid), F32),
            pltpu.VMEM((n_row, tok, hid), BF16),
            pltpu.VMEM((n_row, tok, hid), BF16),
            dma((n_row,)),
            dma((n_row,)),
            dma((n_row,)),
            dma((n_col, per)),
            dma((n_col,)),
            dma((n_col,)),
            dma((n_row,)),
            dma((n_row,)),
        ],
        compiler_params=pltpu.CompilerParams(
            collective_id=0, has_side_effects=True, vmem_limit_bytes=40 << 20
        ),
    )(pair, pair_mask, vec(gin), vec(bin_), wp, vec(bp), wg, vec(bg), vec(gmid), vec(bmid), wo, vec(bo), cot)


def solution(mesh):
    grid = P("row", "col", None)
    placed = (grid, P("row", "col")) + (P(),) * 10 + (grid,)
    return jax.shard_map(
        functools.partial(per_device, mesh.shape["row"], mesh.shape["col"]),
        mesh=mesh,
        in_specs=placed,
        out_specs=(grid, grid),
        check_vma=False,
    )
```

```python
import functools

import jax
import jax.numpy as jnp
from jax import lax
from jax.experimental import pallas as pl
from jax.experimental.pallas import tpu as pltpu
from jax.sharding import PartitionSpec as P

F32 = jnp.float32
BF16 = jnp.bfloat16
MESH = pl.DeviceIdType.MESH


def flip(index, step, size):
    if size & (size - 1):
        return lax.rem(index + step, size)
    partner, weight = 0, 1
    while weight < size:
        mine, other = (index // weight) % 2, (step // weight) % 2
        partner = partner + weight * ((mine + other) % 2)
        weight *= 2
    return partner


def source(index, step, size):
    if size & (size - 1):
        return lax.rem(index + size - step, size)
    return flip(index, step, size)


def normalize(values):
    centred = values - jnp.mean(values, -1, keepdims=True)
    inv_std = lax.rsqrt(jnp.mean(centred * centred, -1, keepdims=True) + 1e-05)
    return centred * inv_std, inv_std


def norm_back(upstream, hat, inv_std, gain):
    scaled = upstream * gain
    return inv_std * (
        scaled
        - jnp.mean(scaled, -1, keepdims=True)
        - hat * jnp.mean(scaled * hat, -1, keepdims=True)
    )


def dot(lhs, rhs):
    return jnp.dot(lhs, rhs, preferred_element_type=F32)


def dot_t(lhs, rhs):
    return lax.dot_general(lhs, rhs, (((1,), (1,)), ((), ())), preferred_element_type=F32)


def kernel(
    n_row, n_col, ti, tj,
    pair_hbm, mask_hbm, gin_hbm, bin_hbm, wp_hbm, bp_hbm, wg_hbm, bg_hbm,
    gmid_hbm, bmid_hbm, wo_hbm, bo_hbm, cot_hbm,
    upd_ref, grad_ref,
    pair_ref, mask_ref, gin_ref, bin_ref, wp_ref, bp_ref, wg_ref, bg_ref,
    gmid_ref, bmid_ref, wo_ref, bo_ref, cot_ref, in_sem,
    stage, a_f, b_out, b_in, b_f, tri_own, tri_out, tri_in, d_out_s, d_in, d_f, gb_own, gb_out, gb_in,
    b_ss, b_rs, t_ss, t_rs, d_ss, d_rs, g_ss, g_rs,
):
    row, col = lax.axis_index("row"), lax.axis_index("col")
    tok = ti * tj
    half = ti * ti
    per = tj // ti
    hid = a_f.shape[-1]

    operands = (
        (pair_hbm, pair_ref), (wp_hbm, wp_ref), (gin_hbm, gin_ref), (bin_hbm, bin_ref),
        (bp_hbm, bp_ref), (mask_hbm, mask_ref), (wg_hbm, wg_ref), (bg_hbm, bg_ref),
        (cot_hbm, cot_ref), (wo_hbm, wo_ref), (gmid_hbm, gmid_ref), (bmid_hbm, bmid_ref),
        (bo_hbm, bo_ref),
    )
    loads = [
        pltpu.make_async_copy(src, dst, in_sem.at[n]) for n, (src, dst) in enumerate(operands)
    ]
    for load in loads:
        load.start()

    barrier = pltpu.get_barrier_semaphore()
    for step in range(1, n_row):
        pl.semaphore_signal(barrier, inc=1, device_id=(flip(row, step, n_row), col), device_id_type=MESH)
    for step in range(1, n_col):
        pl.semaphore_signal(barrier, inc=1, device_id=(row, flip(col, step, n_col)), device_id_type=MESH)

    def reorder(ref):
        stage[...] = ref[...].astype(F32).reshape(tok, hid)
        return jnp.concatenate([stage[pl.ds(k, ti, stride=tj), :] for k in range(tj)], 0)

    loads[0].wait()
    hat_in, rstd_in = normalize(reorder(pair_ref))
    for load in loads[1:6]:
        load.wait()
    x_bf = (hat_in * gin_ref[...] + bin_ref[...]).astype(BF16)
    proj = dot(x_bf, wp_ref[...]) + bp_ref[...]
    mask_v = mask_ref[...].astype(F32)
    mask = jnp.concatenate(
        [jnp.broadcast_to(mask_v[:, k : k + 1], (ti, hid)) for k in range(tj)], 0
    )
    sig_b = jax.nn.sigmoid(proj[:, 2 * hid : 3 * hid])
    val_b = proj[:, 3 * hid :]
    b_bf = (mask * sig_b * val_b).astype(BF16)
    b_out[...] = b_bf

    pl.semaphore_wait(barrier, n_row + n_col - 2)

    def send_b(step):
        to = flip(row, step, n_row)
        return pltpu.make_async_remote_copy(
            b_out, b_in.at[row], b_ss.at[step], b_rs.at[step],
            device_id=(to, col), device_id_type=MESH,
        )

    for step in range(n_row - 1, 0, -1):
        send_b(step).start()

    sig_a = jax.nn.sigmoid(proj[:, :hid])
    val_a = proj[:, hid : 2 * hid]
    a_f[...] = (mask * sig_a * val_a).astype(BF16).astype(F32)
    b_f[row] = b_bf.astype(F32)

    def send_tri(block):
        to = block // per
        part = block % per
        return pltpu.make_async_remote_copy(
            tri_out.at[block], tri_in.at[col, part], t_ss.at[block], t_rs.at[col, part],
            device_id=(row, to), device_id_type=MESH,
        )

    def forward(block):
        sums = []
        a_k = [a_f[k * ti : (k + 1) * ti, :] for k in range(tj)]
        for jj in range(ti):
            total = None
            for k in range(tj):
                term = a_k[k] * b_f[block, k * ti + jj : k * ti + jj + 1, :]
                total = term if total is None else total + term
            sums.append(total)
        whole = jnp.concatenate(sums, 0)

        @pl.when(block // per == col)
        def _():
            tri_own[block % per] = whole

        @pl.when(block // per != col)
        def _():
            tri_out[block] = whole.astype(BF16)
            send_tri(block).start()

    forward(row)

    def forward_step(step, carry):
        block = source(row, step, n_row)
        pltpu.make_async_remote_copy(
            b_out, b_in.at[block], b_ss.at[step], b_rs.at[step],
            device_id=(block, col), device_id_type=MESH,
        ).wait_recv()
        b_f[block] = b_in[block].astype(F32)
        forward(block)
        return carry

    lax.fori_loop(1, n_row, forward_step, 0)

    for load in loads[6:]:
        load.wait()
    gate = jax.nn.sigmoid(dot(x_bf, wg_ref[...]) + bg_ref[...])
    grad_out = reorder(cot_ref)
    d_out = (grad_out * gate).astype(BF16)
    d_mid = dot_t(d_out, wo_ref[...])

    triangle = jnp.concatenate([tri_own[part] for part in range(per)], 0)
    for step in range(1, n_col):
        other = source(col, step, n_col)
        for part in range(per):
            pltpu.make_async_remote_copy(
                tri_out.at[0], tri_in.at[other, part], t_ss.at[0], t_rs.at[other, part],
                device_id=(row, other), device_id_type=MESH,
            ).wait_recv()
        triangle = triangle + jnp.concatenate(
            [tri_in[other, part].astype(F32) for part in range(per)], 0
        )
    hat_mid, rstd_mid = normalize(triangle)
    d_tri = norm_back(d_mid, hat_mid, rstd_mid, gmid_ref[...]).astype(BF16)
    d_out_s[...] = d_tri

    def send_d(step):
        to = flip(col, step, n_col)
        return pltpu.make_async_remote_copy(
            d_out_s, d_in.at[col], d_ss.at[step], d_rs.at[step],
            device_id=(row, to), device_id_type=MESH,
        )

    for step in range(n_col - 1, 0, -1):
        send_d(step).start()
    d_f[pl.ds(col * tok, tok), :] = d_tri.astype(F32)

    def send_gb(block):
        return pltpu.make_async_remote_copy(
            gb_out.at[block], gb_in.at[row], g_ss.at[block], g_rs.at[row],
            device_id=(block, col), device_id_type=MESH,
        )

    def backward_b(block):
        d_i = [d_f[pl.ds(block * half + i, ti, stride=ti), :] for i in range(ti)]
        sums = []
        for k in range(tj):
            total = None
            for i in range(ti):
                term = d_i[i] * a_f[k * ti + i : k * ti + i + 1, :]
                total = term if total is None else total + term
            sums.append(total)
        whole = jnp.concatenate(sums, 0)

        @pl.when(block == row)
        def _():
            gb_own[...] = whole

        @pl.when(block != row)
        def _():
            gb_out[block] = whole.astype(BF16)
            send_gb(block).start()

    for part in range(per):
        backward_b(col * per + part)

    mid_bf = (hat_mid * gmid_ref[...] + bmid_ref[...]).astype(BF16)
    out_lin = dot(mid_bf, wo_ref[...]) + bo_ref[...]
    update = gate * out_lin
    for k in range(tj):
        stage[pl.ds(k, ti, stride=tj), :] = update[k * ti : (k + 1) * ti, :]
    upd_ref[...] = stage[...].astype(BF16).reshape(ti, tj, hid)
    d_gpre = (grad_out * out_lin * gate * (1.0 - gate)).astype(BF16)

    def backward_step(step, carry):
        other = source(col, step, n_col)
        pltpu.make_async_remote_copy(
            d_out_s, d_in.at[other], d_ss.at[step], d_rs.at[step],
            device_id=(row, other), device_id_type=MESH,
        ).wait_recv()
        d_f[pl.ds(other * tok, tok), :] = d_in[other].astype(F32)
        for part in range(per):
            backward_b(other * per + part)
        return carry

    lax.fori_loop(1, n_col, backward_step, 0)

    def backward_a(block, sums):
        out = list(sums)
        for jj in range(ti):
            d_j = d_f[pl.ds(block * half + jj * ti, ti), :]
            for k in range(tj):
                out[k] = out[k] + d_j * b_f[block, k * ti + jj : k * ti + jj + 1, :]
        return tuple(out)

    zero = tuple(jnp.zeros((ti, hid), F32) for _ in range(tj))
    grad_a = jnp.concatenate(lax.fori_loop(0, n_row, backward_a, zero), 0) * mask
    d_ga = (grad_a * val_a * sig_a * (1.0 - sig_a)).astype(BF16)
    d_va = (grad_a * sig_a).astype(BF16)
    d_x = (
        dot_t(d_gpre, wg_ref[...])
        + dot_t(d_ga, wp_ref[:, :hid])
        + dot_t(d_va, wp_ref[:, hid : 2 * hid])
    )

    grad_b = gb_own[...]
    for step in range(1, n_row):
        other = source(row, step, n_row)
        pltpu.make_async_remote_copy(
            gb_out.at[0], gb_in.at[other], g_ss.at[0], g_rs.at[other],
            device_id=(other, col), device_id_type=MESH,
        ).wait_recv()
        grad_b = grad_b + gb_in[other].astype(F32)
    grad_b = grad_b * mask
    d_gb = (grad_b * val_b * sig_b * (1.0 - sig_b)).astype(BF16)
    d_vb = (grad_b * sig_b).astype(BF16)
    d_x = d_x + dot_t(d_gb, wp_ref[:, 2 * hid : 3 * hid]) + dot_t(d_vb, wp_ref[:, 3 * hid :])
    pair_grad = norm_back(d_x, hat_in, rstd_in, gin_ref[...])
    for k in range(tj):
        stage[pl.ds(k, ti, stride=tj), :] = pair_grad[k * ti : (k + 1) * ti, :]
    grad_ref[...] = stage[...].reshape(ti, tj, hid)

    for step in range(1, n_row):
        send_b(step).wait_send()
    for block in range(n_row):
        @pl.when(block // per != col)
        def _():
            send_tri(block).wait_send()
    for step in range(1, n_col):
        send_d(step).wait_send()
    for block in range(n_row):
        @pl.when(block != row)
        def _():
            send_gb(block).wait_send()


def per_device(n_row, n_col, pair, pair_mask, gin, bin_, wp, bp, wg, bg, gmid, bmid, wo, bo, cot):
    ti, tj, chan = pair.shape
    hid = chan
    tok, per = ti * tj, tj // ti
    vec = lambda v: v.reshape(1, -1)
    dma = pltpu.SemaphoreType.DMA
    vmem = pl.BlockSpec(memory_space=pltpu.VMEM)
    operands = (pair, pair_mask, vec(gin), vec(bin_), wp, vec(bp), wg, vec(bg), vec(gmid), vec(bmid), wo, vec(bo), cot)
    return pl.pallas_call(
        functools.partial(kernel, n_row, n_col, ti, tj),
        name="triangle_step",
        out_shape=(
            jax.ShapeDtypeStruct(pair.shape, BF16),
            jax.ShapeDtypeStruct(pair.shape, F32),
        ),
        in_specs=[pl.BlockSpec(memory_space=pltpu.HBM)] * 13,
        out_specs=(vmem, vmem),
        scratch_shapes=[pltpu.VMEM(v.shape, v.dtype) for v in operands]
        + [dma((len(operands),))]
        + [
            pltpu.VMEM((tok, hid), F32),
            pltpu.VMEM((tok, hid), F32),
            pltpu.VMEM((tok, hid), BF16),
            pltpu.VMEM((n_row, tok, hid), BF16),
            pltpu.VMEM((n_row, tok, hid), F32),
            pltpu.VMEM((per, ti * ti, hid), F32),
            pltpu.VMEM((n_row, ti * ti, hid), BF16),
            pltpu.VMEM((n_col, per, ti * ti, hid), BF16),
            pltpu.VMEM((tok, hid), BF16),
            pltpu.VMEM((n_col, tok, hid), BF16),
            pltpu.VMEM((n_col * tok, hid), F32),
            pltpu.VMEM((tok, hid), F32),
            pltpu.VMEM((n_row, tok, hid), BF16),
            pltpu.VMEM((n_row, tok, hid), BF16),
            dma((n_row,)),
            dma((n_row,)),
            dma((n_row,)),
            dma((n_col, per)),
            dma((n_col,)),
            dma((n_col,)),
            dma((n_row,)),
            dma((n_row,)),
        ],
        compiler_params=pltpu.CompilerParams(
            collective_id=0, has_side_effects=True, vmem_limit_bytes=56 << 20
        ),
    )(*operands)


def solution(mesh):
    grid = P("row", "col", None)
    placed = (grid, P("row", "col")) + (P(),) * 10 + (grid,)
    return jax.shard_map(
        functools.partial(per_device, mesh.shape["row"], mesh.shape["col"]),
        mesh=mesh,
        in_specs=placed,
        out_specs=(grid, grid),
        check_vma=False,
    )
```

```python
import functools

import jax
import jax.numpy as jnp
from jax import lax
from jax.experimental import pallas as pl
from jax.experimental.pallas import tpu as pltpu
from jax.sharding import PartitionSpec as P

F32 = jnp.float32
BF16 = jnp.bfloat16
MESH = pl.DeviceIdType.MESH


def flip(index, step, size):
    if size & (size - 1):
        return lax.rem(index + step, size)
    partner, weight = 0, 1
    while weight < size:
        mine, other = (index // weight) % 2, (step // weight) % 2
        partner = partner + weight * ((mine + other) % 2)
        weight *= 2
    return partner


def source(index, step, size):
    if size & (size - 1):
        return lax.rem(index + size - step, size)
    return flip(index, step, size)


def normalize(values):
    centred = values - jnp.mean(values, -1, keepdims=True)
    inv_std = lax.rsqrt(jnp.mean(centred * centred, -1, keepdims=True) + 1e-05)
    return centred * inv_std, inv_std


def norm_back(upstream, hat, inv_std, gain):
    scaled = upstream * gain
    return inv_std * (
        scaled
        - jnp.mean(scaled, -1, keepdims=True)
        - hat * jnp.mean(scaled * hat, -1, keepdims=True)
    )


def dot(lhs, rhs):
    return jnp.dot(lhs, rhs, preferred_element_type=F32)


def dot_t(lhs, rhs):
    return lax.dot_general(lhs, rhs, (((1,), (1,)), ((), ())), preferred_element_type=F32)


def kernel(
    n_row, n_col, ti, tj,
    pair_hbm, mask_hbm, gin_hbm, bin_hbm, wp_hbm, bp_hbm, wg_hbm, bg_hbm,
    gmid_hbm, bmid_hbm, wo_hbm, bo_hbm, cot_hbm,
    upd_ref, grad_ref,
    pair_ref, mask_ref, gin_ref, bin_ref, wp_ref, bp_ref, wg_ref, bg_ref,
    gmid_ref, bmid_ref, wo_ref, bo_ref, cot_ref, in_sem,
    stage, a_f, b_out, b_in, b_f, tri_own, tri_out, tri_in, d_out_s, d_in, d_f, gb_own, gb_out, gb_in,
    b_ss, b_rs, t_ss, t_rs, d_ss, d_rs, g_ss, g_rs,
):
    row, col = lax.axis_index("row"), lax.axis_index("col")
    tok = ti * tj
    half = ti * ti
    per = tj // ti
    hid = a_f.shape[-1]

    operands = (
        (pair_hbm, pair_ref), (wp_hbm, wp_ref), (gin_hbm, gin_ref), (bin_hbm, bin_ref),
        (bp_hbm, bp_ref), (mask_hbm, mask_ref), (wg_hbm, wg_ref), (bg_hbm, bg_ref),
        (cot_hbm, cot_ref), (wo_hbm, wo_ref), (gmid_hbm, gmid_ref), (bmid_hbm, bmid_ref),
        (bo_hbm, bo_ref),
    )
    loads = [
        pltpu.make_async_copy(src, dst, in_sem.at[n]) for n, (src, dst) in enumerate(operands)
    ]
    for load in loads:
        load.start()

    barrier = pltpu.get_barrier_semaphore()
    for step in range(1, n_row):
        pl.semaphore_signal(barrier, inc=1, device_id=(flip(row, step, n_row), col), device_id_type=MESH)
    for step in range(1, n_col):
        pl.semaphore_signal(barrier, inc=1, device_id=(row, flip(col, step, n_col)), device_id_type=MESH)

    def reorder(ref):
        stage[...] = ref[...].astype(F32).reshape(tok, hid)
        return jnp.concatenate([stage[pl.ds(k, ti, stride=tj), :] for k in range(tj)], 0)

    loads[0].wait()
    hat_in, rstd_in = normalize(reorder(pair_ref))
    for load in loads[1:6]:
        load.wait()
    x_bf = (hat_in * gin_ref[...] + bin_ref[...]).astype(BF16)
    proj_b = dot(x_bf, wp_ref[:, 2 * hid :]) + bp_ref[:, 2 * hid :]
    mask_v = mask_ref[...].astype(F32)
    mask = jnp.concatenate(
        [jnp.broadcast_to(mask_v[:, k : k + 1], (ti, hid)) for k in range(tj)], 0
    )
    sig_b = jax.nn.sigmoid(proj_b[:, :hid])
    val_b = proj_b[:, hid:]
    b_bf = (mask * sig_b * val_b).astype(BF16)
    b_out[...] = b_bf

    pl.semaphore_wait(barrier, n_row + n_col - 2)

    def send_b(step):
        to = flip(row, step, n_row)
        return pltpu.make_async_remote_copy(
            b_out, b_in.at[row], b_ss.at[step], b_rs.at[step],
            device_id=(to, col), device_id_type=MESH,
        )

    for step in range(n_row - 1, 0, -1):
        send_b(step).start()

    proj_a = dot(x_bf, wp_ref[:, : 2 * hid]) + bp_ref[:, : 2 * hid]
    sig_a = jax.nn.sigmoid(proj_a[:, :hid])
    val_a = proj_a[:, hid:]
    a_f[...] = (mask * sig_a * val_a).astype(BF16).astype(F32)
    b_f[row] = b_bf.astype(F32)

    def send_tri(block):
        to = block // per
        part = block % per
        return pltpu.make_async_remote_copy(
            tri_out.at[block], tri_in.at[col, part], t_ss.at[block], t_rs.at[col, part],
            device_id=(row, to), device_id_type=MESH,
        )

    def forward(block):
        sums = []
        a_k = [a_f[k * ti : (k + 1) * ti, :] for k in range(tj)]
        for jj in range(ti):
            total = None
            for k in range(tj):
                term = a_k[k] * b_f[block, k * ti + jj : k * ti + jj + 1, :]
                total = term if total is None else total + term
            sums.append(total)
        whole = jnp.concatenate(sums, 0)

        @pl.when(block // per == col)
        def _():
            tri_own[block % per] = whole

        @pl.when(block // per != col)
        def _():
            tri_out[block] = whole.astype(BF16)
            send_tri(block).start()

    forward(row)

    def forward_step(step, carry):
        block = source(row, step, n_row)
        pltpu.make_async_remote_copy(
            b_out, b_in.at[block], b_ss.at[step], b_rs.at[step],
            device_id=(block, col), device_id_type=MESH,
        ).wait_recv()
        b_f[block] = b_in[block].astype(F32)
        forward(block)
        return carry

    lax.fori_loop(1, n_row, forward_step, 0)

    for load in loads[6:]:
        load.wait()
    gate = jax.nn.sigmoid(dot(x_bf, wg_ref[...]) + bg_ref[...])
    grad_out = reorder(cot_ref)
    d_out = (grad_out * gate).astype(BF16)
    d_mid = dot_t(d_out, wo_ref[...])

    triangle = jnp.concatenate([tri_own[part] for part in range(per)], 0)
    for step in range(1, n_col):
        other = source(col, step, n_col)
        for part in range(per):
            pltpu.make_async_remote_copy(
                tri_out.at[0], tri_in.at[other, part], t_ss.at[0], t_rs.at[other, part],
                device_id=(row, other), device_id_type=MESH,
            ).wait_recv()
        triangle = triangle + jnp.concatenate(
            [tri_in[other, part].astype(F32) for part in range(per)], 0
        )
    hat_mid, rstd_mid = normalize(triangle)
    d_tri = norm_back(d_mid, hat_mid, rstd_mid, gmid_ref[...]).astype(BF16)
    d_out_s[...] = d_tri

    def send_d(step):
        to = flip(col, step, n_col)
        return pltpu.make_async_remote_copy(
            d_out_s, d_in.at[col], d_ss.at[step], d_rs.at[step],
            device_id=(row, to), device_id_type=MESH,
        )

    for step in range(n_col - 1, 0, -1):
        send_d(step).start()
    d_f[pl.ds(col * tok, tok), :] = d_tri.astype(F32)

    def send_gb(block):
        return pltpu.make_async_remote_copy(
            gb_out.at[block], gb_in.at[row], g_ss.at[block], g_rs.at[row],
            device_id=(block, col), device_id_type=MESH,
        )

    def backward_b(block):
        d_i = [d_f[pl.ds(block * half + i, ti, stride=ti), :] for i in range(ti)]
        sums = []
        for k in range(tj):
            total = None
            for i in range(ti):
                term = d_i[i] * a_f[k * ti + i : k * ti + i + 1, :]
                total = term if total is None else total + term
            sums.append(total)
        whole = jnp.concatenate(sums, 0)

        @pl.when(block == row)
        def _():
            gb_own[...] = whole

        @pl.when(block != row)
        def _():
            gb_out[block] = whole.astype(BF16)
            send_gb(block).start()

    for part in range(per):
        backward_b(col * per + part)

    mid_bf = (hat_mid * gmid_ref[...] + bmid_ref[...]).astype(BF16)
    out_lin = dot(mid_bf, wo_ref[...]) + bo_ref[...]
    update = gate * out_lin
    for k in range(tj):
        stage[pl.ds(k, ti, stride=tj), :] = update[k * ti : (k + 1) * ti, :]
    upd_ref[...] = stage[...].astype(BF16).reshape(ti, tj, hid)
    d_gpre = (grad_out * out_lin * gate * (1.0 - gate)).astype(BF16)

    def backward_step(step, carry):
        other = source(col, step, n_col)
        pltpu.make_async_remote_copy(
            d_out_s, d_in.at[other], d_ss.at[step], d_rs.at[step],
            device_id=(row, other), device_id_type=MESH,
        ).wait_recv()
        d_f[pl.ds(other * tok, tok), :] = d_in[other].astype(F32)
        for part in range(per):
            backward_b(other * per + part)
        return carry

    lax.fori_loop(1, n_col, backward_step, 0)

    def backward_a(block, sums):
        out = list(sums)
        for jj in range(ti):
            d_j = d_f[pl.ds(block * half + jj * ti, ti), :]
            for k in range(tj):
                out[k] = out[k] + d_j * b_f[block, k * ti + jj : k * ti + jj + 1, :]
        return tuple(out)

    zero = tuple(jnp.zeros((ti, hid), F32) for _ in range(tj))
    grad_a = jnp.concatenate(lax.fori_loop(0, n_row, backward_a, zero), 0) * mask
    d_ga = (grad_a * val_a * sig_a * (1.0 - sig_a)).astype(BF16)
    d_va = (grad_a * sig_a).astype(BF16)
    d_x = (
        dot_t(d_gpre, wg_ref[...])
        + dot_t(d_ga, wp_ref[:, :hid])
        + dot_t(d_va, wp_ref[:, hid : 2 * hid])
    )

    grad_b = gb_own[...]
    for step in range(1, n_row):
        other = source(row, step, n_row)
        pltpu.make_async_remote_copy(
            gb_out.at[0], gb_in.at[other], g_ss.at[0], g_rs.at[other],
            device_id=(other, col), device_id_type=MESH,
        ).wait_recv()
        grad_b = grad_b + gb_in[other].astype(F32)
    grad_b = grad_b * mask
    d_gb = (grad_b * val_b * sig_b * (1.0 - sig_b)).astype(BF16)
    d_vb = (grad_b * sig_b).astype(BF16)
    d_x = d_x + dot_t(d_gb, wp_ref[:, 2 * hid : 3 * hid]) + dot_t(d_vb, wp_ref[:, 3 * hid :])
    pair_grad = norm_back(d_x, hat_in, rstd_in, gin_ref[...])
    for k in range(tj):
        stage[pl.ds(k, ti, stride=tj), :] = pair_grad[k * ti : (k + 1) * ti, :]
    grad_ref[...] = stage[...].reshape(ti, tj, hid)

    for step in range(1, n_row):
        send_b(step).wait_send()
    for block in range(n_row):
        @pl.when(block // per != col)
        def _():
            send_tri(block).wait_send()
    for step in range(1, n_col):
        send_d(step).wait_send()
    for block in range(n_row):
        @pl.when(block != row)
        def _():
            send_gb(block).wait_send()


def store(upd_ref, grad_ref, upd_hbm, grad_hbm, sem):
    first = pltpu.make_async_copy(upd_ref, upd_hbm, sem.at[0])
    second = pltpu.make_async_copy(grad_ref, grad_hbm, sem.at[1])
    second.start()
    first.start()
    second.wait()
    first.wait()


def per_device(n_row, n_col, pair, pair_mask, gin, bin_, wp, bp, wg, bg, gmid, bmid, wo, bo, cot):
    ti, tj, chan = pair.shape
    hid = chan
    tok, per = ti * tj, tj // ti
    vec = lambda v: v.reshape(1, -1)
    dma = pltpu.SemaphoreType.DMA
    vmem = pl.BlockSpec(memory_space=pltpu.VMEM)
    operands = (pair, pair_mask, vec(gin), vec(bin_), wp, vec(bp), wg, vec(bg), vec(gmid), vec(bmid), wo, vec(bo), cot)
    update, grad = pl.pallas_call(
        functools.partial(kernel, n_row, n_col, ti, tj),
        name="triangle_step",
        out_shape=(
            jax.ShapeDtypeStruct(pair.shape, BF16),
            jax.ShapeDtypeStruct(pair.shape, F32),
        ),
        in_specs=[pl.BlockSpec(memory_space=pltpu.HBM)] * 13,
        out_specs=(vmem, vmem),
        scratch_shapes=[pltpu.VMEM(v.shape, v.dtype) for v in operands]
        + [dma((len(operands),))]
        + [
            pltpu.VMEM((tok, hid), F32),
            pltpu.VMEM((tok, hid), F32),
            pltpu.VMEM((tok, hid), BF16),
            pltpu.VMEM((n_row, tok, hid), BF16),
            pltpu.VMEM((n_row, tok, hid), F32),
            pltpu.VMEM((per, ti * ti, hid), F32),
            pltpu.VMEM((n_row, ti * ti, hid), BF16),
            pltpu.VMEM((n_col, per, ti * ti, hid), BF16),
            pltpu.VMEM((tok, hid), BF16),
            pltpu.VMEM((n_col, tok, hid), BF16),
            pltpu.VMEM((n_col * tok, hid), F32),
            pltpu.VMEM((tok, hid), F32),
            pltpu.VMEM((n_row, tok, hid), BF16),
            pltpu.VMEM((n_row, tok, hid), BF16),
            dma((n_row,)),
            dma((n_row,)),
            dma((n_row,)),
            dma((n_col, per)),
            dma((n_col,)),
            dma((n_col,)),
            dma((n_row,)),
            dma((n_row,)),
        ],
        compiler_params=pltpu.CompilerParams(
            collective_id=0, has_side_effects=True, vmem_limit_bytes=40 << 20
        ),
    )(*[pltpu.with_memory_space_constraint(v, pltpu.HBM) for v in operands])
    hbm = pl.BlockSpec(memory_space=pltpu.HBM)
    return pl.pallas_call(
        store,
        name="store_outputs",
        out_shape=(
            jax.ShapeDtypeStruct(pair.shape, BF16),
            jax.ShapeDtypeStruct(pair.shape, F32),
        ),
        in_specs=[vmem, vmem],
        out_specs=(hbm, hbm),
        scratch_shapes=[dma((2,))],
        compiler_params=pltpu.CompilerParams(vmem_limit_bytes=1 << 20),
    )(update, grad)


def solution(mesh):
    grid = P("row", "col", None)
    placed = (grid, P("row", "col")) + (P(),) * 10 + (grid,)
    return jax.shard_map(
        functools.partial(per_device, mesh.shape["row"], mesh.shape["col"]),
        mesh=mesh,
        in_specs=placed,
        out_specs=(grid, grid),
        check_vma=False,
    )
```

```python
import functools

import jax
import jax.numpy as jnp
from jax import lax
from jax.experimental import pallas as pl
from jax.experimental.pallas import tpu as pltpu
from jax.sharding import PartitionSpec as P

F32 = jnp.float32
BF16 = jnp.bfloat16
MESH = pl.DeviceIdType.MESH


def flip(index, step, size):
    if size & (size - 1):
        return lax.rem(index + step, size)
    partner, weight = 0, 1
    while weight < size:
        mine, other = (index // weight) % 2, (step // weight) % 2
        partner = partner + weight * ((mine + other) % 2)
        weight *= 2
    return partner


def source(index, step, size):
    if size & (size - 1):
        return lax.rem(index + size - step, size)
    return flip(index, step, size)


def normalize(values):
    centred = values - jnp.mean(values, -1, keepdims=True)
    inv_std = lax.rsqrt(jnp.mean(centred * centred, -1, keepdims=True) + 1e-05)
    return centred * inv_std, inv_std


def norm_back(upstream, hat, inv_std, gain):
    scaled = upstream * gain
    return inv_std * (
        scaled
        - jnp.mean(scaled, -1, keepdims=True)
        - hat * jnp.mean(scaled * hat, -1, keepdims=True)
    )


def dot(lhs, rhs):
    return jnp.dot(lhs, rhs, preferred_element_type=F32)


def dot_t(lhs, rhs):
    return lax.dot_general(lhs, rhs, (((1,), (1,)), ((), ())), preferred_element_type=F32)


def kernel(
    n_row, n_col, ti, tj,
    pair_hbm, mask_hbm, gin_hbm, bin_hbm, wp_hbm, bp_hbm, wg_hbm, bg_hbm,
    gmid_hbm, bmid_hbm, wo_hbm, bo_hbm, cot_hbm,
    upd_ref, grad_ref,
    pair_ref, mask_ref, gin_ref, bin_ref, wp_ref, bp_ref, wg_ref, bg_ref,
    gmid_ref, bmid_ref, wo_ref, bo_ref, cot_ref, in_sem,
    stage, a_f, b_out, b_in, b_f, tri_own, tri_out, tri_in, d_out_s, d_in, d_f, gb_own, gb_out, gb_in,
    b_ss, b_rs, t_ss, t_rs, d_ss, d_rs, g_ss, g_rs,
):
    row, col = lax.axis_index("row"), lax.axis_index("col")
    tok = ti * tj
    half = ti * ti
    per = tj // ti
    hid = a_f.shape[-1]

    operands = (
        (pair_hbm, pair_ref), (wp_hbm, wp_ref), (gin_hbm, gin_ref), (bin_hbm, bin_ref),
        (bp_hbm, bp_ref), (mask_hbm, mask_ref), (wg_hbm, wg_ref), (bg_hbm, bg_ref),
        (cot_hbm, cot_ref), (wo_hbm, wo_ref), (gmid_hbm, gmid_ref), (bmid_hbm, bmid_ref),
        (bo_hbm, bo_ref),
    )
    loads = [
        pltpu.make_async_copy(src, dst, in_sem.at[n]) for n, (src, dst) in enumerate(operands)
    ]
    for load in loads:
        load.start()

    barrier = pltpu.get_barrier_semaphore()
    for step in range(1, n_row):
        pl.semaphore_signal(barrier, inc=1, device_id=(flip(row, step, n_row), col), device_id_type=MESH)
    for step in range(1, n_col):
        pl.semaphore_signal(barrier, inc=1, device_id=(row, flip(col, step, n_col)), device_id_type=MESH)

    def reorder(ref):
        stage[...] = ref[...].astype(F32).reshape(tok, hid)
        return jnp.concatenate([stage[pl.ds(k, ti, stride=tj), :] for k in range(tj)], 0)

    loads[0].wait()
    hat_in, rstd_in = normalize(reorder(pair_ref))
    for load in loads[1:6]:
        load.wait()
    x_bf = (hat_in * gin_ref[...] + bin_ref[...]).astype(BF16)
    proj_b = dot(x_bf, wp_ref[:, 2 * hid :]) + bp_ref[:, 2 * hid :]
    mask_v = mask_ref[...].astype(F32)
    mask = jnp.concatenate(
        [jnp.broadcast_to(mask_v[:, k : k + 1], (ti, hid)) for k in range(tj)], 0
    )
    sig_b = jax.nn.sigmoid(proj_b[:, :hid])
    val_b = proj_b[:, hid:]
    b_bf = (mask * sig_b * val_b).astype(BF16)
    b_out[...] = b_bf

    pl.semaphore_wait(barrier, n_row + n_col - 2)

    def send_b(step):
        to = flip(row, step, n_row)
        return pltpu.make_async_remote_copy(
            b_out, b_in.at[row], b_ss.at[step], b_rs.at[step],
            device_id=(to, col), device_id_type=MESH,
        )

    for step in range(1, n_row):
        send_b(step).start()

    proj_a = dot(x_bf, wp_ref[:, : 2 * hid]) + bp_ref[:, : 2 * hid]
    sig_a = jax.nn.sigmoid(proj_a[:, :hid])
    val_a = proj_a[:, hid:]
    a_f[...] = (mask * sig_a * val_a).astype(BF16).astype(F32)
    b_f[row] = b_bf.astype(F32)

    def send_tri(block):
        to = block // per
        part = block % per
        return pltpu.make_async_remote_copy(
            tri_out.at[block], tri_in.at[col, part], t_ss.at[block], t_rs.at[col, part],
            device_id=(row, to), device_id_type=MESH,
        )

    def forward(block):
        sums = []
        a_k = [a_f[k * ti : (k + 1) * ti, :] for k in range(tj)]
        for jj in range(ti):
            total = None
            for k in range(tj):
                term = a_k[k] * b_f[block, k * ti + jj : k * ti + jj + 1, :]
                total = term if total is None else total + term
            sums.append(total)
        whole = jnp.concatenate(sums, 0)

        @pl.when(block // per == col)
        def _():
            tri_own[block % per] = whole

        @pl.when(block // per != col)
        def _():
            tri_out[block] = whole.astype(BF16)
            send_tri(block).start()

    forward(row)

    def forward_step(step, carry):
        block = source(row, step, n_row)
        pltpu.make_async_remote_copy(
            b_out, b_in.at[block], b_ss.at[step], b_rs.at[step],
            device_id=(block, col), device_id_type=MESH,
        ).wait_recv()
        b_f[block] = b_in[block].astype(F32)
        forward(block)
        return carry

    lax.fori_loop(1, n_row, forward_step, 0)

    for load in loads[6:]:
        load.wait()
    gate = jax.nn.sigmoid(dot(x_bf, wg_ref[...]) + bg_ref[...])
    grad_out = reorder(cot_ref)
    d_out = (grad_out * gate).astype(BF16)
    d_mid = dot_t(d_out, wo_ref[...])

    triangle = jnp.concatenate([tri_own[part] for part in range(per)], 0)
    for step in range(1, n_col):
        other = source(col, step, n_col)
        for part in range(per):
            pltpu.make_async_remote_copy(
                tri_out.at[0], tri_in.at[other, part], t_ss.at[0], t_rs.at[other, part],
                device_id=(row, other), device_id_type=MESH,
            ).wait_recv()
        triangle = triangle + jnp.concatenate(
            [tri_in[other, part].astype(F32) for part in range(per)], 0
        )
    hat_mid, rstd_mid = normalize(triangle)
    d_tri = norm_back(d_mid, hat_mid, rstd_mid, gmid_ref[...]).astype(BF16)
    d_out_s[...] = d_tri

    def send_d(step):
        to = flip(col, step, n_col)
        return pltpu.make_async_remote_copy(
            d_out_s, d_in.at[col], d_ss.at[step], d_rs.at[step],
            device_id=(row, to), device_id_type=MESH,
        )

    for step in range(n_col - 1, 0, -1):
        send_d(step).start()
    d_f[pl.ds(col * tok, tok), :] = d_tri.astype(F32)

    def send_gb(block):
        return pltpu.make_async_remote_copy(
            gb_out.at[block], gb_in.at[row], g_ss.at[block], g_rs.at[row],
            device_id=(block, col), device_id_type=MESH,
        )

    def backward_b(block):
        d_i = [d_f[pl.ds(block * half + i, ti, stride=ti), :] for i in range(ti)]
        sums = []
        for k in range(tj):
            total = None
            for i in range(ti):
                term = d_i[i] * a_f[k * ti + i : k * ti + i + 1, :]
                total = term if total is None else total + term
            sums.append(total)
        whole = jnp.concatenate(sums, 0)

        @pl.when(block == row)
        def _():
            gb_own[...] = whole

        @pl.when(block != row)
        def _():
            gb_out[block] = whole.astype(BF16)
            send_gb(block).start()

    for part in range(per):
        backward_b(col * per + part)

    mid_bf = (hat_mid * gmid_ref[...] + bmid_ref[...]).astype(BF16)
    out_lin = dot(mid_bf, wo_ref[...]) + bo_ref[...]
    update = gate * out_lin
    for k in range(tj):
        stage[pl.ds(k, ti, stride=tj), :] = update[k * ti : (k + 1) * ti, :]
    upd_ref[...] = stage[...].astype(BF16).reshape(ti, tj, hid)
    d_gpre = (grad_out * out_lin * gate * (1.0 - gate)).astype(BF16)

    def backward_step(step, carry):
        other = source(col, step, n_col)
        pltpu.make_async_remote_copy(
            d_out_s, d_in.at[other], d_ss.at[step], d_rs.at[step],
            device_id=(row, other), device_id_type=MESH,
        ).wait_recv()
        d_f[pl.ds(other * tok, tok), :] = d_in[other].astype(F32)
        for part in range(per):
            backward_b(other * per + part)
        return carry

    lax.fori_loop(1, n_col, backward_step, 0)

    def backward_a(block, sums):
        out = list(sums)
        for jj in range(ti):
            d_j = d_f[pl.ds(block * half + jj * ti, ti), :]
            for k in range(tj):
                out[k] = out[k] + d_j * b_f[block, k * ti + jj : k * ti + jj + 1, :]
        return tuple(out)

    zero = tuple(jnp.zeros((ti, hid), F32) for _ in range(tj))
    grad_a = jnp.concatenate(lax.fori_loop(0, n_row, backward_a, zero), 0) * mask
    d_ga = (grad_a * val_a * sig_a * (1.0 - sig_a)).astype(BF16)
    d_va = (grad_a * sig_a).astype(BF16)
    d_x = (
        dot_t(d_gpre, wg_ref[...])
        + dot_t(d_ga, wp_ref[:, :hid])
        + dot_t(d_va, wp_ref[:, hid : 2 * hid])
    )

    grad_b = gb_own[...]
    for step in range(1, n_row):
        other = source(row, step, n_row)
        pltpu.make_async_remote_copy(
            gb_out.at[0], gb_in.at[other], g_ss.at[0], g_rs.at[other],
            device_id=(other, col), device_id_type=MESH,
        ).wait_recv()
        grad_b = grad_b + gb_in[other].astype(F32)
    grad_b = grad_b * mask
    d_gb = (grad_b * val_b * sig_b * (1.0 - sig_b)).astype(BF16)
    d_vb = (grad_b * sig_b).astype(BF16)
    d_x = d_x + dot_t(d_gb, wp_ref[:, 2 * hid : 3 * hid]) + dot_t(d_vb, wp_ref[:, 3 * hid :])
    pair_grad = norm_back(d_x, hat_in, rstd_in, gin_ref[...])
    for k in range(tj):
        stage[pl.ds(k, ti, stride=tj), :] = pair_grad[k * ti : (k + 1) * ti, :]
    grad_ref[...] = stage[...].reshape(ti, tj, hid)

    for step in range(1, n_row):
        send_b(step).wait_send()
    for block in range(n_row):
        @pl.when(block // per != col)
        def _():
            send_tri(block).wait_send()
    for step in range(1, n_col):
        send_d(step).wait_send()
    for block in range(n_row):
        @pl.when(block != row)
        def _():
            send_gb(block).wait_send()


def store(upd_ref, grad_ref, upd_hbm, grad_hbm, sem):
    first = pltpu.make_async_copy(upd_ref, upd_hbm, sem.at[0])
    second = pltpu.make_async_copy(grad_ref, grad_hbm, sem.at[1])
    second.start()
    first.start()
    second.wait()
    first.wait()


def per_device(n_row, n_col, pair, pair_mask, gin, bin_, wp, bp, wg, bg, gmid, bmid, wo, bo, cot):
    ti, tj, chan = pair.shape
    hid = chan
    tok, per = ti * tj, tj // ti
    vec = lambda v: v.reshape(1, -1)
    dma = pltpu.SemaphoreType.DMA
    vmem = pl.BlockSpec(memory_space=pltpu.VMEM)
    operands = (pair, pair_mask, vec(gin), vec(bin_), wp, vec(bp), wg, vec(bg), vec(gmid), vec(bmid), wo, vec(bo), cot)
    update, grad = pl.pallas_call(
        functools.partial(kernel, n_row, n_col, ti, tj),
        name="triangle_step",
        out_shape=(
            jax.ShapeDtypeStruct(pair.shape, BF16),
            jax.ShapeDtypeStruct(pair.shape, F32),
        ),
        in_specs=[pl.BlockSpec(memory_space=pltpu.HBM)] * 13,
        out_specs=(vmem, vmem),
        scratch_shapes=[pltpu.VMEM(v.shape, v.dtype) for v in operands]
        + [dma((len(operands),))]
        + [
            pltpu.VMEM((tok, hid), F32),
            pltpu.VMEM((tok, hid), F32),
            pltpu.VMEM((tok, hid), BF16),
            pltpu.VMEM((n_row, tok, hid), BF16),
            pltpu.VMEM((n_row, tok, hid), F32),
            pltpu.VMEM((per, ti * ti, hid), F32),
            pltpu.VMEM((n_row, ti * ti, hid), BF16),
            pltpu.VMEM((n_col, per, ti * ti, hid), BF16),
            pltpu.VMEM((tok, hid), BF16),
            pltpu.VMEM((n_col, tok, hid), BF16),
            pltpu.VMEM((n_col * tok, hid), F32),
            pltpu.VMEM((tok, hid), F32),
            pltpu.VMEM((n_row, tok, hid), BF16),
            pltpu.VMEM((n_row, tok, hid), BF16),
            dma((n_row,)),
            dma((n_row,)),
            dma((n_row,)),
            dma((n_col, per)),
            dma((n_col,)),
            dma((n_col,)),
            dma((n_row,)),
            dma((n_row,)),
        ],
        compiler_params=pltpu.CompilerParams(
            collective_id=0, has_side_effects=True, vmem_limit_bytes=40 << 20
        ),
    )(*[pltpu.with_memory_space_constraint(v, pltpu.HBM) for v in operands])
    hbm = pl.BlockSpec(memory_space=pltpu.HBM)
    return pl.pallas_call(
        store,
        name="store_outputs",
        out_shape=(
            jax.ShapeDtypeStruct(pair.shape, BF16),
            jax.ShapeDtypeStruct(pair.shape, F32),
        ),
        in_specs=[vmem, vmem],
        out_specs=(hbm, hbm),
        scratch_shapes=[dma((2,))],
        compiler_params=pltpu.CompilerParams(vmem_limit_bytes=1 << 20),
    )(update, grad)


def solution(mesh):
    grid = P("row", "col", None)
    placed = (grid, P("row", "col")) + (P(),) * 10 + (grid,)
    return jax.shard_map(
        functools.partial(per_device, mesh.shape["row"], mesh.shape["col"]),
        mesh=mesh,
        in_specs=placed,
        out_specs=(grid, grid),
        check_vma=False,
    )
```

```python
import functools

import jax
import jax.numpy as jnp
from jax import lax
from jax.experimental import pallas as pl
from jax.experimental.pallas import tpu as pltpu
from jax.sharding import PartitionSpec as P

F32 = jnp.float32
BF16 = jnp.bfloat16
MESH = pl.DeviceIdType.MESH


def flip(index, step, size):
    if size & (size - 1):
        return lax.rem(index + step, size)
    partner, weight = 0, 1
    while weight < size:
        mine, other = (index // weight) % 2, (step // weight) % 2
        partner = partner + weight * ((mine + other) % 2)
        weight *= 2
    return partner


def source(index, step, size):
    if size & (size - 1):
        return lax.rem(index + size - step, size)
    return flip(index, step, size)


def normalize(values):
    centred = values - jnp.mean(values, -1, keepdims=True)
    inv_std = lax.rsqrt(jnp.mean(centred * centred, -1, keepdims=True) + 1e-05)
    return centred * inv_std, inv_std


def norm_back(upstream, hat, inv_std, gain):
    scaled = upstream * gain
    return inv_std * (
        scaled
        - jnp.mean(scaled, -1, keepdims=True)
        - hat * jnp.mean(scaled * hat, -1, keepdims=True)
    )


def dot(lhs, rhs):
    return jnp.dot(lhs, rhs, preferred_element_type=F32)


def dot_t(lhs, rhs):
    return lax.dot_general(lhs, rhs, (((1,), (1,)), ((), ())), preferred_element_type=F32)


def kernel(
    n_row, n_col, ti, tj,
    pair_hbm, mask_hbm, gin_hbm, bin_hbm, wp_hbm, bp_hbm, wg_hbm, bg_hbm,
    gmid_hbm, bmid_hbm, wo_hbm, bo_hbm, cot_hbm,
    upd_ref, grad_ref,
    pair_ref, mask_ref, gin_ref, bin_ref, wp_ref, bp_ref, wg_ref, bg_ref,
    gmid_ref, bmid_ref, wo_ref, bo_ref, cot_ref, in_sem,
    stage, a_f, b_out, b_in, b_f, tri_own, tri_out, tri_in, d_out_s, d_in, d_f, gb_own, gb_out, gb_in,
    b_ss, b_rs, t_ss, t_rs, d_ss, d_rs, g_ss, g_rs,
):
    row, col = lax.axis_index("row"), lax.axis_index("col")
    tok = ti * tj
    half = ti * ti
    per = tj // ti
    hid = a_f.shape[-1]

    operands = (
        (pair_hbm, pair_ref), (wp_hbm, wp_ref), (gin_hbm, gin_ref), (bin_hbm, bin_ref),
        (bp_hbm, bp_ref), (mask_hbm, mask_ref), (wg_hbm, wg_ref), (bg_hbm, bg_ref),
        (cot_hbm, cot_ref), (wo_hbm, wo_ref), (gmid_hbm, gmid_ref), (bmid_hbm, bmid_ref),
        (bo_hbm, bo_ref),
    )
    loads = [
        pltpu.make_async_copy(src, dst, in_sem.at[n]) for n, (src, dst) in enumerate(operands)
    ]
    for load in loads:
        load.start()

    barrier = pltpu.get_barrier_semaphore()
    for step in range(1, n_row):
        pl.semaphore_signal(barrier, inc=1, device_id=(flip(row, step, n_row), col), device_id_type=MESH)
    for step in range(1, n_col):
        pl.semaphore_signal(barrier, inc=1, device_id=(row, flip(col, step, n_col)), device_id_type=MESH)

    def reorder(ref):
        stage[...] = ref[...].astype(F32).reshape(tok, hid)
        return jnp.concatenate([stage[pl.ds(k, ti, stride=tj), :] for k in range(tj)], 0)

    loads[0].wait()
    hat_in, rstd_in = normalize(reorder(pair_ref))
    for load in loads[1:6]:
        load.wait()
    x_bf = (hat_in * gin_ref[...] + bin_ref[...]).astype(BF16)
    proj_b = dot(x_bf, wp_ref[:, 2 * hid :]) + bp_ref[:, 2 * hid :]
    mask_v = mask_ref[...].astype(F32)
    mask = jnp.concatenate(
        [jnp.broadcast_to(mask_v[:, k : k + 1], (ti, hid)) for k in range(tj)], 0
    )
    sig_b = jax.nn.sigmoid(proj_b[:, :hid])
    val_b = proj_b[:, hid:]
    b_bf = (mask * sig_b * val_b).astype(BF16)
    b_out[...] = b_bf

    pl.semaphore_wait(barrier, n_row + n_col - 2)

    def send_b(step):
        to = flip(row, step, n_row)
        return pltpu.make_async_remote_copy(
            b_out, b_in.at[row], b_ss.at[step], b_rs.at[step],
            device_id=(to, col), device_id_type=MESH,
        )

    for step in range(1, n_row):
        send_b(step).start()

    proj_a = dot(x_bf, wp_ref[:, : 2 * hid]) + bp_ref[:, : 2 * hid]
    sig_a = jax.nn.sigmoid(proj_a[:, :hid])
    val_a = proj_a[:, hid:]
    a_f[...] = (mask * sig_a * val_a).astype(BF16).astype(F32)
    b_f[row] = b_bf.astype(F32)

    def send_tri(block):
        to = block // per
        part = block % per
        return pltpu.make_async_remote_copy(
            tri_out.at[block], tri_in.at[col, part], t_ss.at[block], t_rs.at[col, part],
            device_id=(row, to), device_id_type=MESH,
        )

    def forward(block):
        sums = []
        a_k = [a_f[k * ti : (k + 1) * ti, :] for k in range(tj)]
        for jj in range(ti):
            total = None
            for k in range(tj):
                term = a_k[k] * b_f[block, k * ti + jj : k * ti + jj + 1, :]
                total = term if total is None else total + term
            sums.append(total)
        whole = jnp.concatenate(sums, 0)

        @pl.when(block // per == col)
        def _():
            tri_own[block % per] = whole

        @pl.when(block // per != col)
        def _():
            tri_out[block] = whole.astype(BF16)
            send_tri(block).start()

    forward(row)

    def forward_step(step, carry):
        block = source(row, step, n_row)
        pltpu.make_async_remote_copy(
            b_out, b_in.at[block], b_ss.at[step], b_rs.at[step],
            device_id=(block, col), device_id_type=MESH,
        ).wait_recv()
        b_f[block] = b_in[block].astype(F32)
        forward(block)
        return carry

    lax.fori_loop(1, n_row, forward_step, 0)

    for load in loads[6:]:
        load.wait()
    gate = jax.nn.sigmoid(dot(x_bf, wg_ref[...]) + bg_ref[...])
    grad_out = reorder(cot_ref)
    d_out = (grad_out * gate).astype(BF16)
    d_mid = dot_t(d_out, wo_ref[...])

    triangle = jnp.concatenate([tri_own[part] for part in range(per)], 0)
    for step in range(1, n_col):
        other = source(col, step, n_col)
        for part in range(per):
            pltpu.make_async_remote_copy(
                tri_out.at[0], tri_in.at[other, part], t_ss.at[0], t_rs.at[other, part],
                device_id=(row, other), device_id_type=MESH,
            ).wait_recv()
        triangle = triangle + jnp.concatenate(
            [tri_in[other, part].astype(F32) for part in range(per)], 0
        )
    hat_mid, rstd_mid = normalize(triangle)
    d_tri = norm_back(d_mid, hat_mid, rstd_mid, gmid_ref[...]).astype(BF16)
    d_out_s[...] = d_tri

    def send_d(step):
        to = flip(col, step, n_col)
        return pltpu.make_async_remote_copy(
            d_out_s, d_in.at[col], d_ss.at[step], d_rs.at[step],
            device_id=(row, to), device_id_type=MESH,
        )

    for step in range(1, n_col):
        send_d(step).start()
    d_f[pl.ds(col * tok, tok), :] = d_tri.astype(F32)

    def send_gb(block):
        return pltpu.make_async_remote_copy(
            gb_out.at[block], gb_in.at[row], g_ss.at[block], g_rs.at[row],
            device_id=(block, col), device_id_type=MESH,
        )

    def backward_b(block):
        d_i = [d_f[pl.ds(block * half + i, ti, stride=ti), :] for i in range(ti)]
        sums = []
        for k in range(tj):
            total = None
            for i in range(ti):
                term = d_i[i] * a_f[k * ti + i : k * ti + i + 1, :]
                total = term if total is None else total + term
            sums.append(total)
        whole = jnp.concatenate(sums, 0)

        @pl.when(block == row)
        def _():
            gb_own[...] = whole

        @pl.when(block != row)
        def _():
            gb_out[block] = whole.astype(BF16)
            send_gb(block).start()

    for part in range(per):
        backward_b(col * per + part)

    mid_bf = (hat_mid * gmid_ref[...] + bmid_ref[...]).astype(BF16)
    out_lin = dot(mid_bf, wo_ref[...]) + bo_ref[...]
    update = gate * out_lin
    for k in range(tj):
        stage[pl.ds(k, ti, stride=tj), :] = update[k * ti : (k + 1) * ti, :]
    upd_ref[...] = stage[...].astype(BF16).reshape(ti, tj, hid)
    d_gpre = (grad_out * out_lin * gate * (1.0 - gate)).astype(BF16)

    def backward_step(step, carry):
        other = source(col, step, n_col)
        pltpu.make_async_remote_copy(
            d_out_s, d_in.at[other], d_ss.at[step], d_rs.at[step],
            device_id=(row, other), device_id_type=MESH,
        ).wait_recv()
        d_f[pl.ds(other * tok, tok), :] = d_in[other].astype(F32)
        for part in range(per):
            backward_b(other * per + part)
        return carry

    lax.fori_loop(1, n_col, backward_step, 0)

    def backward_a(block, sums):
        out = list(sums)
        for jj in range(ti):
            d_j = d_f[pl.ds(block * half + jj * ti, ti), :]
            for k in range(tj):
                out[k] = out[k] + d_j * b_f[block, k * ti + jj : k * ti + jj + 1, :]
        return tuple(out)

    zero = tuple(jnp.zeros((ti, hid), F32) for _ in range(tj))
    grad_a = jnp.concatenate(lax.fori_loop(0, n_row, backward_a, zero), 0) * mask
    d_ga = (grad_a * val_a * sig_a * (1.0 - sig_a)).astype(BF16)
    d_va = (grad_a * sig_a).astype(BF16)
    d_x = (
        dot_t(d_gpre, wg_ref[...])
        + dot_t(d_ga, wp_ref[:, :hid])
        + dot_t(d_va, wp_ref[:, hid : 2 * hid])
    )

    grad_b = gb_own[...]
    for step in range(1, n_row):
        other = source(row, step, n_row)
        pltpu.make_async_remote_copy(
            gb_out.at[0], gb_in.at[other], g_ss.at[0], g_rs.at[other],
            device_id=(other, col), device_id_type=MESH,
        ).wait_recv()
        grad_b = grad_b + gb_in[other].astype(F32)
    grad_b = grad_b * mask
    d_gb = (grad_b * val_b * sig_b * (1.0 - sig_b)).astype(BF16)
    d_vb = (grad_b * sig_b).astype(BF16)
    d_x = d_x + dot_t(d_gb, wp_ref[:, 2 * hid : 3 * hid]) + dot_t(d_vb, wp_ref[:, 3 * hid :])
    pair_grad = norm_back(d_x, hat_in, rstd_in, gin_ref[...])
    for k in range(tj):
        stage[pl.ds(k, ti, stride=tj), :] = pair_grad[k * ti : (k + 1) * ti, :]
    grad_ref[...] = stage[...].reshape(ti, tj, hid)

    for step in range(1, n_row):
        send_b(step).wait_send()
    for block in range(n_row):
        @pl.when(block // per != col)
        def _():
            send_tri(block).wait_send()
    for step in range(1, n_col):
        send_d(step).wait_send()
    for block in range(n_row):
        @pl.when(block != row)
        def _():
            send_gb(block).wait_send()


def store(upd_ref, grad_ref, upd_hbm, grad_hbm, sem):
    first = pltpu.make_async_copy(upd_ref, upd_hbm, sem.at[0])
    second = pltpu.make_async_copy(grad_ref, grad_hbm, sem.at[1])
    second.start()
    first.start()
    second.wait()
    first.wait()


def per_device(n_row, n_col, pair, pair_mask, gin, bin_, wp, bp, wg, bg, gmid, bmid, wo, bo, cot):
    ti, tj, chan = pair.shape
    hid = chan
    tok, per = ti * tj, tj // ti
    vec = lambda v: v.reshape(1, -1)
    dma = pltpu.SemaphoreType.DMA
    vmem = pl.BlockSpec(memory_space=pltpu.VMEM)
    operands = (pair, pair_mask, vec(gin), vec(bin_), wp, vec(bp), wg, vec(bg), vec(gmid), vec(bmid), wo, vec(bo), cot)
    update, grad = pl.pallas_call(
        functools.partial(kernel, n_row, n_col, ti, tj),
        name="triangle_step",
        out_shape=(
            jax.ShapeDtypeStruct(pair.shape, BF16),
            jax.ShapeDtypeStruct(pair.shape, F32),
        ),
        in_specs=[pl.BlockSpec(memory_space=pltpu.HBM)] * 13,
        out_specs=(vmem, vmem),
        scratch_shapes=[pltpu.VMEM(v.shape, v.dtype) for v in operands]
        + [dma((len(operands),))]
        + [
            pltpu.VMEM((tok, hid), F32),
            pltpu.VMEM((tok, hid), F32),
            pltpu.VMEM((tok, hid), BF16),
            pltpu.VMEM((n_row, tok, hid), BF16),
            pltpu.VMEM((n_row, tok, hid), F32),
            pltpu.VMEM((per, ti * ti, hid), F32),
            pltpu.VMEM((n_row, ti * ti, hid), BF16),
            pltpu.VMEM((n_col, per, ti * ti, hid), BF16),
            pltpu.VMEM((tok, hid), BF16),
            pltpu.VMEM((n_col, tok, hid), BF16),
            pltpu.VMEM((n_col * tok, hid), F32),
            pltpu.VMEM((tok, hid), F32),
            pltpu.VMEM((n_row, tok, hid), BF16),
            pltpu.VMEM((n_row, tok, hid), BF16),
            dma((n_row,)),
            dma((n_row,)),
            dma((n_row,)),
            dma((n_col, per)),
            dma((n_col,)),
            dma((n_col,)),
            dma((n_row,)),
            dma((n_row,)),
        ],
        compiler_params=pltpu.CompilerParams(
            collective_id=0, has_side_effects=True, vmem_limit_bytes=40 << 20
        ),
    )(*[pltpu.with_memory_space_constraint(v, pltpu.HBM) for v in operands])
    hbm = pl.BlockSpec(memory_space=pltpu.HBM)
    return pl.pallas_call(
        store,
        name="store_outputs",
        out_shape=(
            jax.ShapeDtypeStruct(pair.shape, BF16),
            jax.ShapeDtypeStruct(pair.shape, F32),
        ),
        in_specs=[vmem, vmem],
        out_specs=(hbm, hbm),
        scratch_shapes=[dma((2,))],
        compiler_params=pltpu.CompilerParams(vmem_limit_bytes=1 << 20),
    )(update, grad)


def solution(mesh):
    grid = P("row", "col", None)
    placed = (grid, P("row", "col")) + (P(),) * 10 + (grid,)
    return jax.shard_map(
        functools.partial(per_device, mesh.shape["row"], mesh.shape["col"]),
        mesh=mesh,
        in_specs=placed,
        out_specs=(grid, grid),
        check_vma=False,
    )
```
